256 devices in a mesh: seq: 32 (over z, y), head: 4 (over x), dp: 2 (over core).
Axes of the slice: x: 4, y: 4, z: 8, core: 2. Of those that a mesh axis runs over, the one named last changes fastest.
Arguments:
- x_in: bfloat16 [16384, 8192], P(('dp', 'seq'), 'head'), parts along dimension 0, as said below
- bc_in: bfloat16 [16384, 2048], P(('dp', 'seq'), 'head'), parts along dimension 0, may hold values from -6 to 6
- z_in: bfloat16 [16384, 8192], P(('dp', 'seq'), 'head'), parts along dimension 0, may hold values from -6 to 6
- dt_raw: float32 [16384, 128], P(('dp', 'seq'), 'head'), parts along dimension 0, as said below
- dt_bias: float32 [128], P('head'), as said below
- a_log: float32 [128], P('head'), as said below
- d_skip: float32 [128], P('head'), may hold values from 0.5 to 1.5
- conv_x: float32 [4, 8192], P(None, 'head'), may hold values from -3 to 3
- conv_bc: float32 [4, 2048], P(None, 'head'), may hold values from -3 to 3
- norm_gain: float32 [8192], P('head'), may hold values from 0.1 to 1.9
- out_weight: bfloat16 [8192, 4096], P('head', 'seq'), may hold values from -0.125 to 0.125
Outputs:
- layer_out: bfloat16 [16384, 4096], P(('dp', 'seq'), 'head'), parts along dimension 0
The draws below stay inside these ranges and needn't reach their ends.
There are 2 independent parts, one for each index of `dp`. The reference program is written for one: setup_inputs(seed, part) draws one part's arguments, and reference() takes and returns one part's arrays. A program takes and returns all parts, laid end to end along the dimension named above; an argument that names none is the same for every part. Nothing has to cross between parts.
Inputs may be any that keep to these rules, and one draw needn't show every extreme that they name: `x_in`: finite values. `dt_raw`: finite values. `dt_bias`: finite values. `a_log`: finite values.
All inputs are finite; a program needn't handle non-finite values.
Results may differ from the reference program's by a relative error of at most 0.0051.
Values may be sent and summed in bfloat16 or wider, within the bound.
No kernel may reach another device: no remote copies, remote signals or barrier semaphores. Data moves between devices by JAX's collectives and lax.ppermute only.
A program may use at most 192 MiB of HBM per device.

```python
import math
import jax
import jax.numpy as jnp
from jax import lax

D = 4096
H = 128
P_SIZE = 64
N = 128
G = 8
BLOCK = 256
CONV = 4
LETTERS_PER_PART = 256
DI = 8192
LETTER_TOTAL = 8192


def head_rates(key):
    folded = jax.random.fold_in(key, 11)
    pick_key, slow_key, fast_key = jax.random.split(folded, 3)
    spread_key = jax.random.fold_in(key, 13)
    slow_heads = jax.random.uniform(pick_key, (H,)) < 0.5
    slow_rate = jax.random.uniform(slow_key, (H,), jnp.float32, 0.3, 0.75)
    fast_rate = jax.random.uniform(fast_key, (H,), jnp.float32, 0.7, 1.4)
    head_factor = jnp.exp(jax.random.uniform(spread_key, (H,), jnp.float32, -0.7, 0.7))
    window = max(BLOCK // 6, 2)
    slow_step = 2.0 / math.sqrt(LETTER_TOTAL * N)
    fast_step = 2.0 / math.sqrt(window * N)
    step_base = jnp.where(slow_heads, slow_step, fast_step) * head_factor
    decay_rate = jnp.where(slow_heads, slow_rate / LETTER_TOTAL, fast_rate / window) / step_base
    return (step_base, decay_rate)


def spike_markers(key):
    spots = jax.random.randint(jax.random.fold_in(key, 23), (2,), CONV, LETTER_TOTAL)
    places = jnp.arange(LETTER_TOTAL, dtype=jnp.int32)
    agreement_tally = jnp.any(places[:, None] == spots[None, :], axis=1)
    adjacent_lines = jnp.any((places[:, None] >= spots[None, :] - (CONV - 1)) & (places[:, None] <= spots[None, :]), axis=1)
    return (agreement_tally, adjacent_lines)


def draw_a_log(key, part):
    step_base, decay_rate = head_rates(key)
    return jnp.log(decay_rate).astype(jnp.float32)


def draw_dt_bias(key, part):
    step_base, decay_rate = head_rates(key)
    return jnp.log(jnp.expm1(step_base)).astype(jnp.float32)


def draw_dt_raw(key, part):
    agreement_tally, adjacent_lines = spike_markers(key)
    noise_key, level_key = jax.random.split(jax.random.fold_in(key, 5))
    noise = 0.5 * jnp.clip(jax.random.normal(noise_key, (LETTER_TOTAL, H), jnp.float32), -4.0, 4.0)
    levels = jax.random.uniform(level_key, (LETTER_TOTAL // LETTERS_PER_PART, 1), jnp.float32, -0.7, 0.7)
    levels = jnp.repeat(levels, LETTERS_PER_PART, axis=0)
    jump = jnp.where(agreement_tally, math.log(0.8 * LETTER_TOTAL), 0.0)[:, None]
    return (noise + levels + jump).astype(jnp.float32)


def draw_x_in(key, part):
    agreement_tally, adjacent_lines = spike_markers(key)
    value_key = jax.random.fold_in(jax.random.fold_in(key, 7), 0)
    values = jax.random.normal(value_key, (LETTER_TOTAL, H * P_SIZE), jnp.float32)
    values = values * jnp.where(adjacent_lines, 0.001, 1.0)[:, None]
    return values.astype(jnp.bfloat16)


def with_spikes(entries, rng, source, target, blocks, factor):
    owner, partner = [(jnp.arange(entries.shape[position]) // (entries.shape[position] // blocks)).reshape([-1 if axis == position else 1 for axis in range(entries.ndim)]) for position in (source, target)]
    chosen = jax.random.permutation(rng, blocks)[partner]
    strong = (owner == chosen) | (owner == (partner + blocks // 2) % blocks)
    return jnp.where(strong, factor * entries, entries)


def level_of(stream_key, shape, cuts, least, largest):
    factor_of, own = 1.0, jax.random.fold_in(stream_key, 6)
    for axis_at, shards_of in cuts:
        steps = jnp.exp(jax.random.uniform(jax.random.fold_in(own, axis_at), (shards_of,), jnp.float32, least / len(cuts), largest / len(cuts)))
        factor_of = factor_of * jnp.repeat(steps, shape[axis_at] // shards_of).reshape([-1 if axis == axis_at else 1 for axis in range(len(shape))])
    return factor_of


def gaussian(key, extent, width, limit, cuts=(), kind=jnp.bfloat16):
    array = width * jax.random.normal(key, extent, jnp.float32)
    if cuts:
        array = array * level_of(key, extent, cuts, -0.22, 0.18)
    return jnp.clip(array, -limit, limit).astype(kind)


def gaussian_with(rng, dims, scale, limit, pieces, heavy, held_as=jnp.bfloat16):
    result = scale * jax.random.normal(rng, dims, jnp.float32)
    if pieces:
        result = result * level_of(rng, dims, pieces, -0.22, 0.18)
    return jnp.clip(with_spikes(result, jax.random.fold_in(rng, 3), *heavy), -limit, limit).astype(held_as)


def setup_inputs(seed: int = 0, part: int = 0) -> dict:
    keys = jax.random.split(jax.random.key(seed), 12)
    part_splits = jax.random.split(jax.random.fold_in(keys[11], part), 12)
    x_in = draw_x_in(jax.random.fold_in(jax.random.fold_in(keys[11], part), 71), part)
    bc_in = gaussian(part_splits[1], (LETTER_TOTAL, G * 2 * N), 1.0, 6.0, ((0, 32), (1, 4)))
    z_in = gaussian(part_splits[2], (LETTER_TOTAL, DI), 1.0, 6.0, ((0, 32), (1, 4)))
    dt_raw = draw_dt_raw(jax.random.fold_in(jax.random.fold_in(keys[11], part), 71), part)
    dt_bias = draw_dt_bias(jax.random.fold_in(keys[11], 71), part)
    a_log = draw_a_log(jax.random.fold_in(keys[11], 71), part)
    d_skip = jnp.clip(0.5 + 1.0 * jax.random.uniform(keys[6], (H,), jnp.float32) ** level_of(keys[6], (H,), ((0, 4),), -0.2, 0.2), 0.5, 1.5)
    conv_x = gaussian(keys[7], (CONV, DI), 0.5, 3.0, ((1, 4),), jnp.float32)
    conv_bc = gaussian(keys[8], (CONV, G * 2 * N), 0.5, 3.0, ((1, 4),), jnp.float32)
    norm_gain = jnp.clip(1.0 + 0.18 * jax.random.normal(keys[9], (DI,), jnp.float32), 0.1, 1.9)
    out_weight = gaussian_with(keys[10], (DI, D), DI ** -0.5, 0.125, ((0, 4), (1, 32)), (0, 1, 32, 2.75))
    return dict(x_in=x_in, bc_in=bc_in, z_in=z_in, dt_raw=dt_raw, dt_bias=dt_bias, a_log=a_log, d_skip=d_skip, conv_x=conv_x, conv_bc=conv_bc, norm_gain=norm_gain, out_weight=out_weight)


epsilon = 1e-05

def causal_conv(values, weight):
    length = values.shape[0]
    padded = jnp.concatenate([jnp.zeros((CONV - 1, values.shape[1]), jnp.float32), values], axis=0)
    summed = jnp.zeros(values.shape, jnp.float32)
    for offset in range(CONV):
        summed = summed + weight[offset][None, :] * padded[offset:offset + length]
    return summed

def reference(x_in, bc_in, z_in, dt_raw, dt_bias, a_log, d_skip, conv_x, conv_bc, norm_gain, out_weight):
    input_convolved = jax.nn.silu(causal_conv(x_in.astype(jnp.float32), conv_x)).astype(jnp.bfloat16)
    bc_conv = jax.nn.silu(causal_conv(bc_in.astype(jnp.float32), conv_bc)).astype(jnp.bfloat16)
    step_sizes = jax.nn.softplus(dt_raw + dt_bias[None, :])
    log_decay = -jnp.exp(a_log)[None, :] * step_sizes
    blocks = LETTER_TOTAL // BLOCK
    per_group = H // G
    bc_groups = bc_conv.reshape(LETTER_TOTAL, G, 2, N)
    b_mat = bc_groups[:, :, 0]
    c_mat = bc_groups[:, :, 1]
    x_blocks = input_convolved.reshape(blocks, BLOCK, H, P_SIZE)
    b_blocks = b_mat.reshape(blocks, BLOCK, G, N)
    c_blocks = c_mat.reshape(blocks, BLOCK, G, N)
    decay_blocks = log_decay.reshape(blocks, BLOCK, H)
    step_blocks = step_sizes.reshape(blocks, BLOCK, H)
    places = jnp.arange(BLOCK, dtype=jnp.int32)
    lower = places[:, None] >= places[None, :]

    def advance(state, input_rows):
        x_here, b_here, c_here, decay_here, step_here = input_rows
        running = jnp.cumsum(decay_here, axis=0)
        scores = jnp.einsum('ign,jgn->gij', c_here.astype(jnp.float32), b_here.astype(jnp.float32))
        score_heads = jnp.repeat(scores, per_group, axis=0)
        running_heads = running.T
        spread = running_heads[:, :, None] - running_heads[:, None, :]
        spread = jnp.where(lower[None], spread, -jnp.inf)
        mixing = (score_heads * jnp.exp(spread) * step_here.T[:, None, :]).astype(jnp.bfloat16)
        within = jnp.einsum('hij,jhp->ihp', mixing.astype(jnp.float32), x_here.astype(jnp.float32))
        until_finish = jnp.exp(running[-1][None, :] - running) * step_here
        b_heads = jnp.repeat(b_here.astype(jnp.float32), per_group, axis=1)
        weighted_b = (b_heads * until_finish[:, :, None]).astype(jnp.bfloat16)
        fresh = jnp.einsum('jhn,jhp->hnp', weighted_b.astype(jnp.float32), x_here.astype(jnp.float32))
        since_beginning = jnp.repeat(c_here.astype(jnp.float32), per_group, axis=1) * jnp.exp(running)[:, :, None]
        across = jnp.einsum('ihn,hnp->ihp', since_beginning, state, precision=lax.Precision.HIGHEST)
        mixed = within + across + d_skip[None, :, None] * x_here.astype(jnp.float32)
        state = jnp.exp(running[-1])[:, None, None] * state + fresh
        return (state, mixed.reshape(BLOCK, H * P_SIZE))
    start_state = jnp.zeros((H, N, P_SIZE), jnp.float32)
    unused, outputs = lax.scan(advance, start_state, (x_blocks, b_blocks, c_blocks, decay_blocks, step_blocks))
    mixed = outputs.reshape(LETTER_TOTAL, H * P_SIZE)
    gated = mixed * jax.nn.silu(z_in.astype(jnp.float32))
    mean_square = lax.optimization_barrier(jnp.mean(gated * gated, axis=1, keepdims=True))
    normed = (gated * lax.rsqrt(mean_square + epsilon) * norm_gain[None, :]).astype(jnp.bfloat16)
    layer_out = jnp.dot(normed, out_weight, preferred_element_type=jnp.float32)
    return layer_out.astype(jnp.bfloat16)
```

```python
import jax
import jax.numpy as jnp
from jax import lax
from jax.experimental import pallas as pl
from jax.experimental.pallas import tpu as pltpu
from jax.sharding import PartitionSpec as P

H = 128
P_SIZE = 64
N = 128
BLOCK = 256
CONV = 4
SLAB = 128
HALO = 8
EPSILON = 1e-05

bf16 = jnp.bfloat16
f32 = jnp.float32


def pieces_of(value):
    high = value.astype(bf16)
    rest = value - high.astype(f32)
    middle = rest.astype(bf16)
    low = (rest - middle.astype(f32)).astype(bf16)
    return high, middle, low


def silu(value):
    return value / (1.0 + jnp.exp(-value))


def convolved(halo, current, taps):
    joined = jnp.concatenate([halo.astype(f32), current.astype(f32)], axis=0)
    height = current.shape[0]
    first = HALO - (CONV - 1)
    summed = taps[0:1] * joined[first : first + height]
    for k in range(1, CONV):
        summed = summed + taps[k : k + 1] * joined[first + k : first + k + height]
    return silu(summed).astype(bf16)


def spread_pair(left, right, rows):
    lane = lax.broadcasted_iota(jnp.int32, (rows, SLAB), 1)
    return jnp.where(
        lane < P_SIZE,
        jnp.broadcast_to(left, (rows, SLAB)),
        jnp.broadcast_to(right, (rows, SLAB)),
    )


def front_kernel(
    x_ref, bc_ref, halo_ref, dt_ref, bias_ref, alog_ref, tapx_ref, tapbc_ref,
    xc_ref, bcv_ref, col_ref, row_ref, send_ref,
):
    heads = dt_ref.shape[0]
    width = x_ref.shape[1]
    raw = dt_ref[...] + bias_ref[...]
    step = jnp.maximum(raw, 0.0) + jnp.log1p(jnp.exp(-jnp.abs(raw)))
    running = -jnp.exp(alog_ref[...]) * step
    lane = lax.broadcasted_iota(jnp.int32, running.shape, 1)
    shift = 1
    while shift < BLOCK:
        moved = pltpu.roll(running, shift, 1)
        running = running + jnp.where(lane >= shift, moved, 0.0)
        shift *= 2
    finish = jnp.exp(running[:, BLOCK - 1 : BLOCK] - running) * step
    row_ref[0:heads] = running
    row_ref[heads : 2 * heads] = step
    columns = jnp.concatenate([running, step, finish, jnp.exp(running)], axis=0).T
    col_ref[...] = columns

    groups = bc_ref.shape[1] // (2 * N)
    turned = []
    for g in range(2 * groups):
        at = slice(g * N, (g + 1) * N)
        here = convolved(halo_ref[:, width + g * N : width + (g + 1) * N], bc_ref[:, at], tapbc_ref[:, at])
        bcv_ref[:, at] = here
        if g % 2 == 0:
            turned.append(here.astype(f32).T.astype(bf16))
    slabs = width // SLAB
    for c in range(slabs):
        at = slice(c * SLAB, (c + 1) * SLAB)
        here = convolved(halo_ref[:, at], x_ref[:, at], tapx_ref[:, at])
        xc_ref[:, at] = here
        h = 2 * c
        weight = spread_pair(
            columns[:, 2 * heads + h : 2 * heads + h + 1],
            columns[:, 2 * heads + h + 1 : 2 * heads + h + 2],
            BLOCK,
        )
        weighted = (here.astype(f32) * weight).astype(bf16)
        fresh = jnp.dot(turned[c // (slabs // groups)], weighted, preferred_element_type=f32)
        decay = spread_pair(
            columns[BLOCK - 1 : BLOCK, 3 * heads + h : 3 * heads + h + 1],
            columns[BLOCK - 1 : BLOCK, 3 * heads + h + 1 : 3 * heads + h + 2],
            8,
        )
        high, middle, low = pieces_of(decay)
        sub = lax.broadcasted_iota(jnp.int32, (8, SLAB), 0)
        lines = jnp.where(
            sub == 0, high.astype(f32), jnp.where(sub == 1, middle.astype(f32), low.astype(f32))
        ).astype(bf16)
        send_ref[2 * c, 0 : N // 2] = fresh[0 : N // 2].astype(bf16)
        send_ref[2 * c + 1, 0 : N // 2] = fresh[N // 2 : N].astype(bf16)
        send_ref[2 * c, N // 2 : N // 2 + 8] = lines
        send_ref[2 * c + 1, N // 2 : N // 2 + 8] = lines


def scan_kernel(got_ref, start_ref):
    count = got_ref.shape[0]
    rows = start_ref.shape[1]

    def advance(j, state):
        start_ref[j] = state.astype(bf16)
        block = got_ref[j].astype(f32)
        decay = block[rows : rows + 1] + block[rows + 1 : rows + 2] + block[rows + 2 : rows + 3]
        return decay * state + block[0:rows]

    lax.fori_loop(0, count, advance, jnp.zeros((rows, SLAB), f32))


def within_kernel(xc_ref, bcv_ref, col_ref, row_ref, skip_ref, out_ref):
    heads = row_ref.shape[0] // 2
    slabs = xc_ref.shape[1] // SLAB
    groups = bcv_ref.shape[1] // (2 * N)
    half = BLOCK // 2
    lane = lax.broadcasted_iota(jnp.int32, (half, SLAB), 1)
    sub = lax.broadcasted_iota(jnp.int32, (half, half), 0)
    across_lane = lax.broadcasted_iota(jnp.int32, (half, half), 1)
    keep = sub >= across_lane
    for g in range(groups):
        b_here = bcv_ref[:, 2 * g * N : (2 * g + 1) * N]
        c_here = bcv_ref[:, (2 * g + 1) * N : (2 * g + 2) * N]
        scores = lax.dot_general(
            c_here, b_here, (((1,), (1,)), ((), ())), preferred_element_type=f32
        )
        for c in range(g * slabs // groups, (g + 1) * slabs // groups):
            at = slice(c * SLAB, (c + 1) * SLAB)
            x_here = xc_ref[:, at]
            parts = []
            for h in (2 * c, 2 * c + 1):
                run_row = row_ref[h : h + 1]
                step_row = row_ref[heads + h : heads + h + 1]
                run_col = jnp.broadcast_to(col_ref[:, h : h + 1], (BLOCK, half))

                def mix(i, j, run_col=run_col, run_row=run_row, step_row=step_row):
                    ri = slice(i * half, (i + 1) * half)
                    rj = slice(j * half, (j + 1) * half)
                    spread = run_col[ri] - run_row[:, rj]
                    if i == j:
                        spread = jnp.where(keep, spread, -jnp.inf)
                    return (scores[ri, rj] * jnp.exp(spread) * step_row[:, rj]).astype(bf16)

                upper = jnp.dot(mix(0, 0), x_here[0:half], preferred_element_type=f32)
                lower = jnp.dot(
                    jnp.concatenate([mix(1, 0), mix(1, 1)], axis=1),
                    x_here,
                    preferred_element_type=f32,
                )
                parts.append((upper, lower))
            skip = skip_ref[:, at]
            for i in range(2):
                ri = slice(i * half, (i + 1) * half)
                out_ref[ri, at] = (
                    jnp.where(lane < P_SIZE, parts[0][i], parts[1][i])
                    + skip * x_here[ri].astype(f32)
                )


def gate_kernel(within_ref, state_ref, bcv_ref, col_ref, z_ref, gain_ref, out_ref, tail_ref):
    heads = col_ref.shape[1] // 4
    slabs = within_ref.shape[1] // SLAB
    groups = bcv_ref.shape[1] // (2 * N)
    squares = jnp.zeros((BLOCK, SLAB), f32)
    for c in range(slabs):
        at = slice(c * SLAB, (c + 1) * SLAB)
        g = c // (slabs // groups)
        c_here = bcv_ref[:, (2 * g + 1) * N : (2 * g + 2) * N]
        across = jnp.dot(c_here, state_ref[c], preferred_element_type=f32)
        h = 3 * heads + 2 * c
        grown = spread_pair(col_ref[:, h : h + 1], col_ref[:, h + 1 : h + 2], BLOCK)
        mixed = within_ref[:, at] + across * grown
        gated = mixed * silu(z_ref[:, at].astype(f32))
        squares = squares + gated * gated
        out_ref[:, at] = (gated * gain_ref[:, at]).astype(bf16)
    line = lax.dot_general(
        jnp.ones((8, SLAB), f32),
        squares,
        (((1,), (1,)), ((), ())),
        preferred_element_type=f32,
        precision=lax.Precision.HIGHEST,
    )
    high, middle, low = pieces_of(line)
    tail_ref[:, 0:BLOCK] = high
    tail_ref[:, BLOCK : 2 * BLOCK] = middle
    tail_ref[:, 2 * BLOCK : 3 * BLOCK] = low
    tail_ref[:, 3 * BLOCK : 4 * BLOCK] = jnp.zeros((8, BLOCK), bf16)


def project_kernel(which_ref, own_ref, other_ref, tail_ref, w_own_ref, w_other_ref, out_ref):
    total = jnp.dot(own_ref[...], w_own_ref[...], preferred_element_type=f32)
    total = total + jnp.dot(other_ref[...], w_other_ref[...], preferred_element_type=f32)
    out_ref[0, 0:BLOCK] = total.astype(bf16)
    out_ref[0, BLOCK : BLOCK + 8] = tail_ref[...]


def finish_kernel(got_ref, out_ref):
    count = got_ref.shape[0]
    total = got_ref[0, 0:BLOCK].astype(f32)
    for k in range(1, count):
        total = total + got_ref[k, 0:BLOCK].astype(f32)
    line = jnp.zeros((8, BLOCK), f32)
    for k in range(count):
        for i in range(3):
            line = line + got_ref[k, BLOCK : BLOCK + 8, i * BLOCK : (i + 1) * BLOCK].astype(f32)
    scale = lax.rsqrt(line / (H * P_SIZE) + EPSILON)
    column = jnp.concatenate([scale] * 16, axis=0).T[:, 0:1]
    out_ref[...] = (total * column).astype(bf16)


def whole(count):
    return [pl.BlockSpec(memory_space=pltpu.VMEM) for _ in range(count)]


def shards(
    x_in, bc_in, z_in, dt_raw, dt_bias, a_log, d_skip, conv_x, conv_bc, norm_gain, out_weight
):
    height, width = x_in.shape
    heads = dt_raw.shape[1]
    nearby = bc_in.shape[1]
    slabs = width // SLAB
    count = lax.axis_size("seq")
    fans = lax.axis_size("head")
    columns = out_weight.shape[1] * count
    rows = width // 2
    core = lax.axis_index("dp")

    w_half = lax.dynamic_slice_in_dim(out_weight, core * rows, rows, 0)
    w_own = lax.all_gather(w_half, "seq", axis=1, tiled=True)
    tail = jnp.concatenate([x_in[height - HALO :], bc_in[height - HALO :]], axis=1)
    halo = lax.ppermute(tail, "seq", [(i, i + 1) for i in range(count - 1)])

    xc, bcv, cols, lines, send = pl.pallas_call(
        front_kernel,
        out_shape=(
            jax.ShapeDtypeStruct((height, width), bf16),
            jax.ShapeDtypeStruct((height, nearby), bf16),
            jax.ShapeDtypeStruct((height, 4 * heads), f32),
            jax.ShapeDtypeStruct((2 * heads, height), f32),
            jax.ShapeDtypeStruct((2 * slabs, N // 2 + 8, SLAB), bf16),
        ),
        in_specs=whole(8),
        out_specs=tuple(whole(5)),
        name="front",
    )(x_in, bc_in, halo, dt_raw.T, dt_bias[:, None], a_log[:, None], conv_x, conv_bc)

    got = lax.all_to_all(send, "seq", 0, 0, tiled=True)
    starts = pl.pallas_call(
        scan_kernel,
        out_shape=jax.ShapeDtypeStruct((count, N // 2, SLAB), bf16),
        in_specs=whole(1),
        out_specs=whole(1)[0],
        name="carry",
    )(got)
    state = lax.all_to_all(starts, "seq", 0, 0, tiled=True).reshape(slabs, N, SLAB)
    w_own, state = lax.optimization_barrier((w_own, state))
    w_other = lax.ppermute(w_own, "dp", [(0, 1), (1, 0)])

    within = pl.pallas_call(
        within_kernel,
        out_shape=jax.ShapeDtypeStruct((height, width), f32),
        in_specs=whole(5),
        out_specs=whole(1)[0],
        name="within",
    )(xc, bcv, cols, lines, jnp.repeat(d_skip, P_SIZE)[None])

    ready, squares = pl.pallas_call(
        gate_kernel,
        out_shape=(
            jax.ShapeDtypeStruct((height, width), bf16),
            jax.ShapeDtypeStruct((8, columns // fans), bf16),
        ),
        in_specs=whole(6),
        out_specs=tuple(whole(2)),
        name="gate",
    )(within, state, bcv, cols, z_in, norm_gain[None])

    share = columns // fans
    partial = pl.pallas_call(
        project_kernel,
        grid_spec=pltpu.PrefetchScalarGridSpec(
            num_scalar_prefetch=1,
            grid=(fans,),
            in_specs=[
                pl.BlockSpec((height, rows), lambda j, s: (0, s[0])),
                pl.BlockSpec((height, rows), lambda j, s: (0, 1 - s[0])),
                pl.BlockSpec((8, share), lambda j, s: (0, 0)),
                pl.BlockSpec((rows, share), lambda j, s: (0, j)),
                pl.BlockSpec((rows, share), lambda j, s: (0, j)),
            ],
            out_specs=pl.BlockSpec((1, height + 8, share), lambda j, s: (j, 0, 0)),
        ),
        out_shape=jax.ShapeDtypeStruct((fans, height + 8, share), bf16),
        name="project",
    )(core.astype(jnp.int32)[None], ready, ready, squares, w_own, w_other)

    swapped = lax.all_to_all(partial, "head", 0, 0, tiled=True)
    return pl.pallas_call(
        finish_kernel,
        out_shape=jax.ShapeDtypeStruct((height, share), bf16),
        in_specs=whole(1),
        out_specs=whole(1)[0],
        name="finish",
    )(swapped)


def solution(mesh):
    placed = (
        P(("dp", "seq"), "head"),
        P(("dp", "seq"), "head"),
        P(("dp", "seq"), "head"),
        P(("dp", "seq"), "head"),
        P("head"),
        P("head"),
        P("head"),
        P(None, "head"),
        P(None, "head"),
        P("head"),
        P("head", "seq"),
    )
    return jax.shard_map(
        shards, mesh=mesh, in_specs=placed, out_specs=P(("dp", "seq"), "head"), check_vma=False
    )
```

```python
import jax
import jax.numpy as jnp
from jax import lax
from jax.experimental import pallas as pl
from jax.experimental.pallas import tpu as pltpu
from jax.sharding import PartitionSpec as P

H = 128
P_SIZE = 64
N = 128
BLOCK = 256
CONV = 4
SLAB = 128
HALO = 8
TAIL = 8
EPSILON = 1e-05

bf16 = jnp.bfloat16
f32 = jnp.float32


def pieces_of(value):
    high = value.astype(bf16)
    rest = value - high.astype(f32)
    middle = rest.astype(bf16)
    low = (rest - middle.astype(f32)).astype(bf16)
    return high, middle, low


def silu(value):
    return value / (1.0 + jnp.exp(-value))


def convolved(halo, current, taps):
    joined = jnp.concatenate([halo.astype(f32), current.astype(f32)], axis=0)
    height = current.shape[0]
    first = HALO - (CONV - 1)
    summed = taps[0:1] * joined[first : first + height]
    for k in range(1, CONV):
        summed = summed + taps[k : k + 1] * joined[first + k : first + k + height]
    return silu(summed).astype(bf16)


def spread_pair(left, right, rows):
    lane = lax.broadcasted_iota(jnp.int32, (rows, SLAB), 1)
    return jnp.where(
        lane < P_SIZE,
        jnp.broadcast_to(left, (rows, SLAB)),
        jnp.broadcast_to(right, (rows, SLAB)),
    )


def front_kernel(
    x_ref, bc_ref, halo_ref, dt_ref, bias_ref, alog_ref, tapx_ref, tapbc_ref,
    xc_ref, bcv_ref, col_ref, row_ref, send_ref,
):
    heads = dt_ref.shape[0]
    width = x_ref.shape[1]
    diagonal = lax.broadcasted_iota(jnp.int32, (heads, heads), 0) == lax.broadcasted_iota(
        jnp.int32, (heads, heads), 1
    )

    def stood(line):
        square = jnp.broadcast_to(line, (heads, heads))
        return jnp.sum(jnp.where(diagonal, square, 0.0), axis=1, keepdims=True)

    raw = dt_ref[...] + stood(bias_ref[...])
    step = jnp.maximum(raw, 0.0) + jnp.log1p(jnp.exp(-jnp.abs(raw)))
    running = -jnp.exp(stood(alog_ref[...])) * step
    lane = lax.broadcasted_iota(jnp.int32, running.shape, 1)
    shift = 1
    while shift < BLOCK:
        moved = pltpu.roll(running, shift, 1)
        running = running + jnp.where(lane >= shift, moved, 0.0)
        shift *= 2
    finish = jnp.exp(running[:, BLOCK - 1 : BLOCK] - running) * step
    row_ref[0:heads] = running
    row_ref[heads : 2 * heads] = step
    columns = jnp.concatenate([running, step, finish, jnp.exp(running)], axis=0).T
    col_ref[...] = columns

    groups = bc_ref.shape[1] // (2 * N)
    turned = []
    for g in range(2 * groups):
        at = slice(g * N, (g + 1) * N)
        here = convolved(halo_ref[:, width + g * N : width + (g + 1) * N], bc_ref[:, at], tapbc_ref[:, at])
        bcv_ref[:, at] = here
        if g % 2 == 0:
            turned.append(here.astype(f32).T.astype(bf16))
    slabs = width // SLAB
    for c in range(slabs):
        at = slice(c * SLAB, (c + 1) * SLAB)
        here = convolved(halo_ref[:, at], x_ref[:, at], tapx_ref[:, at])
        xc_ref[:, at] = here
        h = 2 * c
        weight = spread_pair(
            columns[:, 2 * heads + h : 2 * heads + h + 1],
            columns[:, 2 * heads + h + 1 : 2 * heads + h + 2],
            BLOCK,
        )
        weighted = (here.astype(f32) * weight).astype(bf16)
        fresh = jnp.dot(turned[c // (slabs // groups)], weighted, preferred_element_type=f32)
        decay = spread_pair(
            columns[BLOCK - 1 : BLOCK, 3 * heads + h : 3 * heads + h + 1],
            columns[BLOCK - 1 : BLOCK, 3 * heads + h + 1 : 3 * heads + h + 2],
            8,
        )
        high, middle, low = pieces_of(decay)
        sub = lax.broadcasted_iota(jnp.int32, (8, SLAB), 0)
        lines = jnp.where(
            sub == 0, high.astype(f32), jnp.where(sub == 1, middle.astype(f32), low.astype(f32))
        ).astype(bf16)
        send_ref[2 * c, 0 : N // 2] = fresh[0 : N // 2].astype(bf16)
        send_ref[2 * c + 1, 0 : N // 2] = fresh[N // 2 : N].astype(bf16)
        send_ref[2 * c, N // 2 : N // 2 + 8] = lines
        send_ref[2 * c + 1, N // 2 : N // 2 + 8] = lines


def scan_kernel(got_ref, start_ref):
    count = got_ref.shape[0]
    rows = start_ref.shape[1]

    def advance(j, state):
        start_ref[j] = state.astype(bf16)
        block = got_ref[j].astype(f32)
        decay = block[rows : rows + 1] + block[rows + 1 : rows + 2] + block[rows + 2 : rows + 3]
        return decay * state + block[0:rows]

    lax.fori_loop(0, count, advance, jnp.zeros((rows, SLAB), f32))


def within_kernel(xc_ref, bcv_ref, col_ref, row_ref, skip_ref, out_ref):
    heads = row_ref.shape[0] // 2
    slabs = xc_ref.shape[1] // SLAB
    groups = bcv_ref.shape[1] // (2 * N)
    half = BLOCK // 2
    lane = lax.broadcasted_iota(jnp.int32, (half, SLAB), 1)
    sub = lax.broadcasted_iota(jnp.int32, (half, half), 0)
    across_lane = lax.broadcasted_iota(jnp.int32, (half, half), 1)
    keep = sub >= across_lane
    for g in range(groups):
        b_here = bcv_ref[:, 2 * g * N : (2 * g + 1) * N]
        c_here = bcv_ref[:, (2 * g + 1) * N : (2 * g + 2) * N]
        scores = lax.dot_general(
            c_here, b_here, (((1,), (1,)), ((), ())), preferred_element_type=f32
        )
        for c in range(g * slabs // groups, (g + 1) * slabs // groups):
            at = slice(c * SLAB, (c + 1) * SLAB)
            x_here = xc_ref[:, at]
            parts = []
            for h in (2 * c, 2 * c + 1):
                run_row = row_ref[h : h + 1]
                step_row = row_ref[heads + h : heads + h + 1]
                run_col = jnp.broadcast_to(col_ref[:, h : h + 1], (BLOCK, half))

                def mix(i, j, run_col=run_col, run_row=run_row, step_row=step_row):
                    ri = slice(i * half, (i + 1) * half)
                    rj = slice(j * half, (j + 1) * half)
                    spread = run_col[ri] - run_row[:, rj]
                    if i == j:
                        spread = jnp.where(keep, spread, -jnp.inf)
                    return (scores[ri, rj] * jnp.exp(spread) * step_row[:, rj]).astype(bf16)

                upper = jnp.dot(mix(0, 0), x_here[0:half], preferred_element_type=f32)
                lower = jnp.dot(
                    jnp.concatenate([mix(1, 0), mix(1, 1)], axis=1),
                    x_here,
                    preferred_element_type=f32,
                )
                parts.append((upper, lower))
            skip = skip_ref[:, at]
            for i in range(2):
                ri = slice(i * half, (i + 1) * half)
                out_ref[ri, at] = (
                    jnp.where(lane < P_SIZE, parts[0][i], parts[1][i])
                    + skip * x_here[ri].astype(f32)
                )


def gate_kernel(within_ref, state_ref, bcv_ref, col_ref, z_ref, gain_ref, out_ref):
    heads = col_ref.shape[1] // 4
    slabs = within_ref.shape[1] // SLAB
    groups = bcv_ref.shape[1] // (2 * N)
    squares = jnp.zeros((BLOCK, SLAB), f32)
    for c in range(slabs):
        at = slice(c * SLAB, (c + 1) * SLAB)
        g = c // (slabs // groups)
        c_here = bcv_ref[:, (2 * g + 1) * N : (2 * g + 2) * N]
        across = jnp.dot(c_here, state_ref[c], preferred_element_type=f32)
        h = 3 * heads + 2 * c
        grown = spread_pair(col_ref[:, h : h + 1], col_ref[:, h + 1 : h + 2], BLOCK)
        mixed = within_ref[:, at] + across * grown
        gated = mixed * silu(z_ref[:, at].astype(f32))
        squares = squares + gated * gated
        out_ref[0:BLOCK, at] = (gated * gain_ref[:, at]).astype(bf16)
    line = lax.dot_general(
        jnp.ones((TAIL, SLAB), f32),
        squares,
        (((1,), (1,)), ((), ())),
        preferred_element_type=f32,
        precision=lax.Precision.HIGHEST,
    )
    end = slice(BLOCK, BLOCK + TAIL)
    out_ref[end, 2 * BLOCK :] = jnp.zeros((TAIL, within_ref.shape[1] - 2 * BLOCK), bf16)
    for i, piece in enumerate(pieces_of(line)[0:2]):
        out_ref[end, i * BLOCK : (i + 1) * BLOCK] = piece


def turn_kernel(core_ref, w_ref, out_ref, turned_ref):
    turned_ref[...] = w_ref[...].astype(f32).T
    rows = out_ref.shape[0]
    first = pl.multiple_of(core_ref[0] * rows, rows)
    out_ref[...] = turned_ref[pl.ds(first, rows)].astype(bf16)


def against(left, right):
    return lax.dot_general(left, right, (((1,), (1,)), ((), ())), preferred_element_type=f32)


def project_kernel(core_ref, own_ref, other_ref, w_ref, out_ref):
    core = core_ref[0]
    end = slice(BLOCK, BLOCK + TAIL)
    for seat, ref in ((core, own_ref), (1 - core, other_ref)):
        out_ref[seat, 0:BLOCK] = against(ref[0:BLOCK], w_ref[...]).astype(bf16)
        out_ref[seat, end] = ref[end, 0 : 2 * BLOCK]


def finish_kernel(got_ref, out_ref):
    sources = got_ref.shape[0]
    end = slice(BLOCK, BLOCK + TAIL)
    line = jnp.zeros((TAIL, BLOCK), f32)
    for k in range(0, sources, 2):
        for i in range(2):
            line = line + got_ref[k, end, i * BLOCK : (i + 1) * BLOCK].astype(f32)
    scale = lax.rsqrt(line / (H * P_SIZE) + EPSILON)
    column = jnp.concatenate([scale] * (SLAB // TAIL), axis=0).T[:, 0:1]
    scale = jnp.broadcast_to(column, (BLOCK, SLAB))
    lane = lax.broadcasted_iota(jnp.int32, (BLOCK, SLAB), 1)
    half = SLAB // 2
    for m in range(got_ref.shape[2] // SLAB):
        at = slice(m * SLAB, (m + 1) * SLAB)
        sums = []
        for d in range(2):
            total = got_ref[d, 0:BLOCK, at].astype(f32)
            for k in range(d + 2, sources, 2):
                total = total + got_ref[k, 0:BLOCK, at].astype(f32)
            sums.append(total * scale)
        first = jnp.where(lane < half, sums[0], pltpu.roll(sums[1], half, 1))
        second = jnp.where(lane < half, pltpu.roll(sums[0], half, 1), sums[1])
        out_ref[:, 2 * m * SLAB : (2 * m + 1) * SLAB] = first.astype(bf16)
        out_ref[:, (2 * m + 1) * SLAB : (2 * m + 2) * SLAB] = second.astype(bf16)


def whole(count):
    return [pl.BlockSpec(memory_space=pltpu.VMEM) for _ in range(count)]


def shards(
    x_in, bc_in, z_in, dt_raw, dt_bias, a_log, d_skip, conv_x, conv_bc, norm_gain, out_weight
):
    height, width = x_in.shape
    heads = dt_raw.shape[1]
    nearby = bc_in.shape[1]
    slabs = width // SLAB
    count = lax.axis_size("seq")
    fans = lax.axis_size("head")
    core = lax.axis_index("dp")

    tail = jnp.concatenate([x_in[height - HALO :], bc_in[height - HALO :]], axis=1)
    halo = lax.ppermute(tail, "seq", [(i, i + 1) for i in range(count - 1)])

    seat = core.astype(jnp.int32)[None]
    piece_rows = out_weight.shape[1] // 2
    piece = pl.pallas_call(
        turn_kernel,
        out_shape=jax.ShapeDtypeStruct((piece_rows, width), bf16),
        in_specs=[pl.BlockSpec(memory_space=pltpu.SMEM)] + whole(1),
        out_specs=whole(1)[0],
        scratch_shapes=[pltpu.VMEM((2 * piece_rows, width), f32)],
        name="turn",
    )(seat, out_weight)
    weights = lax.all_gather(piece, "seq", axis=0, tiled=True)

    xc, bcv, cols, lines, send = pl.pallas_call(
        front_kernel,
        out_shape=(
            jax.ShapeDtypeStruct((height, width), bf16),
            jax.ShapeDtypeStruct((height, nearby), bf16),
            jax.ShapeDtypeStruct((height, 4 * heads), f32),
            jax.ShapeDtypeStruct((2 * heads, height), f32),
            jax.ShapeDtypeStruct((2 * slabs, N // 2 + 8, SLAB), bf16),
        ),
        in_specs=whole(8),
        out_specs=tuple(whole(5)),
        name="front",
    )(x_in, bc_in, halo, dt_raw.T, dt_bias[None], a_log[None], conv_x, conv_bc)

    got = lax.all_to_all(send, "seq", 0, 0, tiled=True)
    starts = pl.pallas_call(
        scan_kernel,
        out_shape=jax.ShapeDtypeStruct((count, N // 2, SLAB), bf16),
        in_specs=whole(1),
        out_specs=whole(1)[0],
        name="carry",
    )(got)
    state = lax.all_to_all(starts, "seq", 0, 0, tiled=True).reshape(slabs, N, SLAB)

    within = pl.pallas_call(
        within_kernel,
        out_shape=jax.ShapeDtypeStruct((height, width), f32),
        in_specs=whole(5),
        out_specs=whole(1)[0],
        name="within",
    )(xc, bcv, cols, lines, jnp.repeat(d_skip, P_SIZE)[None])

    ready = pl.pallas_call(
        gate_kernel,
        out_shape=jax.ShapeDtypeStruct((height + TAIL, width), bf16),
        in_specs=whole(6),
        out_specs=whole(1)[0],
        name="gate",
    )(within, state, bcv, cols, z_in, norm_gain[None])

    other = lax.ppermute(ready, "dp", [(0, 1), (1, 0)])
    share = piece_rows * count // fans
    partial = pl.pallas_call(
        project_kernel,
        grid_spec=pltpu.PrefetchScalarGridSpec(
            num_scalar_prefetch=1,
            grid=(fans,),
            in_specs=[
                pl.BlockSpec((height + TAIL, width), lambda j, s: (0, 0)),
                pl.BlockSpec((height + TAIL, width), lambda j, s: (0, 0)),
                pl.BlockSpec((share, width), lambda j, s: (j, 0)),
            ],
            out_specs=pl.BlockSpec((2, height + TAIL, share), lambda j, s: (j, 0, 0)),
        ),
        out_shape=jax.ShapeDtypeStruct((2 * fans, height + TAIL, share), bf16),
        name="project",
    )(seat, ready, other, weights)

    swapped = lax.all_to_all(partial, ("head", "dp"), 0, 0, tiled=True)
    return pl.pallas_call(
        finish_kernel,
        out_shape=jax.ShapeDtypeStruct((height, 2 * share), bf16),
        in_specs=whole(1),
        out_specs=whole(1)[0],
        name="finish",
    )(swapped)


def solution(mesh):
    placed = (
        P(("dp", "seq"), "head"),
        P(("dp", "seq"), "head"),
        P(("dp", "seq"), "head"),
        P(("dp", "seq"), "head"),
        P("head"),
        P("head"),
        P("head"),
        P(None, "head"),
        P(None, "head"),
        P("head"),
        P("head", "seq"),
    )
    return jax.shard_map(
        shards, mesh=mesh, in_specs=placed, out_specs=P(("dp", "seq"), "head"), check_vma=False
    )
```

```python
import jax
import jax.numpy as jnp
from jax import lax
from jax.experimental import pallas as pl
from jax.experimental.pallas import tpu as pltpu
from jax.sharding import PartitionSpec as P


H = 128
P_SIZE = 64
N = 128
BLOCK = 256
CONV = 4
SLAB = 128
HALO = 8
TAIL = 8
EPSILON = 1e-05


bf16 = jnp.bfloat16
f32 = jnp.float32


def pieces_of(value):
    high = value.astype(bf16)
    rest = value - high.astype(f32)
    middle = rest.astype(bf16)
    low = (rest - middle.astype(f32)).astype(bf16)
    return high, middle, low


def silu(value):
    return value / (1.0 + jnp.exp(-value))


def convolved(halo, current, taps):
    joined = jnp.concatenate([halo.astype(f32), current.astype(f32)], axis=0)
    height = current.shape[0]
    first = HALO - (CONV - 1)
    summed = taps[0:1] * joined[first : first + height]
    for k in range(1, CONV):
        summed = summed + taps[k : k + 1] * joined[first + k : first + k + height]
    return silu(summed).astype(bf16)


def spread_pair(left, right, rows):
    lane = lax.broadcasted_iota(jnp.int32, (rows, SLAB), 1)
    return jnp.where(
        lane < P_SIZE,
        jnp.broadcast_to(left, (rows, SLAB)),
        jnp.broadcast_to(right, (rows, SLAB)),
    )


def front_kernel(
    x_ref, bc_ref, halo_ref, dt_ref, bias_ref, alog_ref, tapx_ref, tapbc_ref,
    xc_ref, bcv_ref, col_ref, row_ref, send_ref,
):
    heads = dt_ref.shape[0]
    width = x_ref.shape[1]
    diagonal = lax.broadcasted_iota(jnp.int32, (heads, heads), 0) == lax.broadcasted_iota(
        jnp.int32, (heads, heads), 1
    )

    def stood(line):
        square = jnp.broadcast_to(line, (heads, heads))
        return jnp.sum(jnp.where(diagonal, square, 0.0), axis=1, keepdims=True)

    raw = dt_ref[...] + stood(bias_ref[...])
    step = jnp.maximum(raw, 0.0) + jnp.log1p(jnp.exp(-jnp.abs(raw)))
    running = -jnp.exp(stood(alog_ref[...])) * step
    lane = lax.broadcasted_iota(jnp.int32, running.shape, 1)
    shift = 1
    while shift < BLOCK:
        moved = pltpu.roll(running, shift, 1)
        running = running + jnp.where(lane >= shift, moved, 0.0)
        shift *= 2
    finish = jnp.exp(running[:, BLOCK - 1 : BLOCK] - running) * step
    row_ref[0:heads] = running
    row_ref[heads : 2 * heads] = step
    columns = jnp.concatenate([running, step, finish, jnp.exp(running)], axis=0).T
    col_ref[...] = columns

    groups = bc_ref.shape[1] // (2 * N)
    turned = []
    for g in range(2 * groups):
        at = slice(g * N, (g + 1) * N)
        here = convolved(halo_ref[:, width + g * N : width + (g + 1) * N], bc_ref[:, at], tapbc_ref[:, at])
        bcv_ref[:, at] = here
        if g % 2 == 0:
            turned.append(here.astype(f32).T.astype(bf16))
    slabs = width // SLAB
    for c in range(slabs):
        at = slice(c * SLAB, (c + 1) * SLAB)
        here = convolved(halo_ref[:, at], x_ref[:, at], tapx_ref[:, at])
        xc_ref[:, at] = here
        h = 2 * c
        weight = spread_pair(
            columns[:, 2 * heads + h : 2 * heads + h + 1],
            columns[:, 2 * heads + h + 1 : 2 * heads + h + 2],
            BLOCK,
        )
        weighted = (here.astype(f32) * weight).astype(bf16)
        fresh = jnp.dot(turned[c // (slabs // groups)], weighted, preferred_element_type=f32)
        decay = spread_pair(
            columns[BLOCK - 1 : BLOCK, 3 * heads + h : 3 * heads + h + 1],
            columns[BLOCK - 1 : BLOCK, 3 * heads + h + 1 : 3 * heads + h + 2],
            8,
        )
        high, middle, low = pieces_of(decay)
        sub = lax.broadcasted_iota(jnp.int32, (8, SLAB), 0)
        lines = jnp.where(
            sub == 0, high.astype(f32), jnp.where(sub == 1, middle.astype(f32), low.astype(f32))
        ).astype(bf16)
        send_ref[2 * c, 0 : N // 2] = fresh[0 : N // 2].astype(bf16)
        send_ref[2 * c + 1, 0 : N // 2] = fresh[N // 2 : N].astype(bf16)
        send_ref[2 * c, N // 2 : N // 2 + 8] = lines
        send_ref[2 * c + 1, N // 2 : N // 2 + 8] = lines


def scan_kernel(got_ref, start_ref):
    count = got_ref.shape[0]
    rows = start_ref.shape[1]

    def advance(j, state):
        start_ref[j] = state.astype(bf16)
        block = got_ref[j].astype(f32)
        decay = block[rows : rows + 1] + block[rows + 1 : rows + 2] + block[rows + 2 : rows + 3]
        return decay * state + block[0:rows]

    lax.fori_loop(0, count, advance, jnp.zeros((rows, SLAB), f32))


def within_kernel(xc_ref, bcv_ref, col_ref, row_ref, skip_ref, out_ref):
    heads = row_ref.shape[0] // 2
    slabs = xc_ref.shape[1] // SLAB
    groups = bcv_ref.shape[1] // (2 * N)
    half = BLOCK // 2
    lane = lax.broadcasted_iota(jnp.int32, (half, SLAB), 1)
    sub = lax.broadcasted_iota(jnp.int32, (half, half), 0)
    across_lane = lax.broadcasted_iota(jnp.int32, (half, half), 1)
    keep = sub >= across_lane
    for g in range(groups):
        b_here = bcv_ref[:, 2 * g * N : (2 * g + 1) * N]
        c_here = bcv_ref[:, (2 * g + 1) * N : (2 * g + 2) * N]
        scores = lax.dot_general(
            c_here, b_here, (((1,), (1,)), ((), ())), preferred_element_type=f32
        )
        for c in range(g * slabs // groups, (g + 1) * slabs // groups):
            at = slice(c * SLAB, (c + 1) * SLAB)
            x_here = xc_ref[:, at]
            parts = []
            for h in (2 * c, 2 * c + 1):
                run_row = row_ref[h : h + 1]
                step_row = row_ref[heads + h : heads + h + 1]
                run_col = jnp.broadcast_to(col_ref[:, h : h + 1], (BLOCK, half))

                def mix(i, j, run_col=run_col, run_row=run_row, step_row=step_row):
                    ri = slice(i * half, (i + 1) * half)
                    rj = slice(j * half, (j + 1) * half)
                    spread = run_col[ri] - run_row[:, rj]
                    if i == j:
                        spread = jnp.where(keep, spread, -jnp.inf)
                    return (scores[ri, rj] * jnp.exp(spread) * step_row[:, rj]).astype(bf16)

                upper = jnp.dot(mix(0, 0), x_here[0:half], preferred_element_type=f32)
                lower = jnp.dot(
                    jnp.concatenate([mix(1, 0), mix(1, 1)], axis=1),
                    x_here,
                    preferred_element_type=f32,
                )
                parts.append((upper, lower))
            skip = skip_ref[:, at]
            for i in range(2):
                ri = slice(i * half, (i + 1) * half)
                out_ref[ri, at] = (
                    jnp.where(lane < P_SIZE, parts[0][i], parts[1][i])
                    + skip * x_here[ri].astype(f32)
                )


def gate_kernel(within_ref, state_ref, bcv_ref, col_ref, z_ref, gain_ref, out_ref):
    heads = col_ref.shape[1] // 4
    slabs = within_ref.shape[1] // SLAB
    groups = bcv_ref.shape[1] // (2 * N)
    squares = jnp.zeros((BLOCK, SLAB), f32)
    for c in range(slabs):
        at = slice(c * SLAB, (c + 1) * SLAB)
        g = c // (slabs // groups)
        c_here = bcv_ref[:, (2 * g + 1) * N : (2 * g + 2) * N]
        across = jnp.dot(c_here, state_ref[c], preferred_element_type=f32)
        h = 3 * heads + 2 * c
        grown = spread_pair(col_ref[:, h : h + 1], col_ref[:, h + 1 : h + 2], BLOCK)
        mixed = within_ref[:, at] + across * grown
        gated = mixed * silu(z_ref[:, at].astype(f32))
        squares = squares + gated * gated
        out_ref[0:BLOCK, at] = (gated * gain_ref[:, at]).astype(bf16)
    line = lax.dot_general(
        jnp.ones((TAIL, SLAB), f32),
        squares,
        (((1,), (1,)), ((), ())),
        preferred_element_type=f32,
        precision=lax.Precision.HIGHEST,
    )
    end = slice(BLOCK, BLOCK + TAIL)
    for i, piece in enumerate(pieces_of(line)):
        out_ref[end, i * BLOCK : (i + 1) * BLOCK] = piece
    rest = within_ref.shape[1] - 3 * BLOCK
    out_ref[end, 3 * BLOCK :] = jnp.zeros((TAIL, rest), bf16)


def project_kernel(place_ref, *refs):
    sides = (refs[0:5], refs[5:10])
    w_refs = refs[10:12]
    outs = refs[12:14]
    totals = refs[14:16]
    left_ref, done = refs[16:18]
    k = pl.program_id(0)
    depth = w_refs[0].shape[0]
    tall = BLOCK + TAIL
    half = BLOCK // 2
    spans = ((0, 0, tall), (1, 0, tall), (2, 0, tall), (3, 0, half), (3, half, half + TAIL))
    copies = [
        pltpu.make_async_copy(
            side[i], left_ref.at[step, n, pl.ds(first, count)], done.at[n, i]
        )
        for n, side in enumerate(sides)
        for i, (step, first, count) in enumerate(spans)
    ]

    @pl.when(k == 0)
    def _():
        for i in (0, 5, 1, 6, 2, 7, 3, 8, 4, 9):
            copies[i].start()

    for step in range(4):

        @pl.when(k == step)
        def _(step=step):
            for i in (step, 4) if step == 3 else (step,):
                copies[i].wait()
                copies[5 + i].wait()

    @pl.when(k == 0)
    def _():
        for total in totals:
            total[...] = jnp.zeros(total.shape, f32)

    for r in range(2):
        weight = jnp.concatenate(
            [w_ref[:, (2 * j + r) * SLAB : (2 * j + r + 1) * SLAB] for w_ref in w_refs for j in range(2)],
            axis=1,
        )
        at = slice(r * depth, (r + 1) * depth)
        for n, total in enumerate(totals):
            total[...] = total[...] + jnp.dot(
                left_ref[k, n, 0:BLOCK, at], weight, preferred_element_type=f32
            )

    @pl.when(k == 3)
    def _():
        end = slice(BLOCK, tall)
        for n, (total, out) in enumerate(zip(totals, outs)):
            line = jnp.zeros((TAIL, BLOCK), f32)
            for step in range(4):
                for i in range(3):
                    line = line + left_ref[step, n, end, i * BLOCK : (i + 1) * BLOCK].astype(f32)
            scale = lax.rsqrt(line / (H * P_SIZE) + EPSILON)
            column = jnp.concatenate([scale] * (SLAB // TAIL), axis=0).T[:, 0:1]
            out[...] = (total[...] * column).astype(bf16)


def finish_kernel(core_ref, mine_ref, theirs_ref, out_ref):
    core = core_ref[0]
    for j in range(mine_ref.shape[1] // SLAB):
        at = slice(j * SLAB, (j + 1) * SLAB)
        mine = pl.multiple_of((2 * j + core) * SLAB, SLAB)
        theirs = pl.multiple_of((2 * j + 1 - core) * SLAB, SLAB)
        out_ref[:, pl.ds(mine, SLAB)] = mine_ref[:, at]
        out_ref[:, pl.ds(theirs, SLAB)] = theirs_ref[:, at]


def seat_of(h, half, x):
    away = (x - h) % 4
    return (2 * h + (1 + away if half else -away)) % 8


def weight_route(fans):
    ring = 4
    route = []
    for h in range(fans):
        for half in range(2):
            for x in range(fans):
                for y in range(ring):
                    for core in range(2):
                        source = (((2 * h + half) * ring + y) * fans + x) * 2 + core
                        seat = seat_of(h, half, x) * ring + 2 * (y // 2) + core
                        route.append((source, (seat * fans + h) * 2 + y % 2))
    return route


def whole(count):
    return [pl.BlockSpec(memory_space=pltpu.VMEM) for _ in range(count)]


def layer(
    x_in, bc_in, z_in, dt_raw, dt_bias, a_log, d_skip, conv_x, conv_bc, norm_gain, out_weight
):
    height, width = x_in.shape
    heads = dt_raw.shape[1]
    nearby = bc_in.shape[1]
    slabs = width // SLAB
    count = lax.axis_size("seq")
    fans = lax.axis_size("head")
    core = lax.axis_index("dp")
    mine = lax.axis_index("head")

    tail = jnp.concatenate([x_in[height - HALO :], bc_in[height - HALO :]], axis=1)
    halo = lax.ppermute(tail, "seq", [(i, i + 1) for i in range(count - 1)])

    depth = width // 2
    piece = lax.dynamic_slice_in_dim(out_weight, core * depth, depth, 0)
    piece = lax.ppermute(piece, ("seq", "head", "dp"), weight_route(fans))

    xc, bcv, cols, lines, send = pl.pallas_call(
        front_kernel,
        out_shape=(
            jax.ShapeDtypeStruct((height, width), bf16),
            jax.ShapeDtypeStruct((height, nearby), bf16),
            jax.ShapeDtypeStruct((height, 4 * heads), f32),
            jax.ShapeDtypeStruct((2 * heads, height), f32),
            jax.ShapeDtypeStruct((2 * slabs, N // 2 + 8, SLAB), bf16),
        ),
        in_specs=whole(8),
        out_specs=tuple(whole(5)),
        name="front",
    )(x_in, bc_in, halo, dt_raw.T, dt_bias[None], a_log[None], conv_x, conv_bc)

    weights = lax.all_gather(piece, "seq", axis=1, tiled=True)
    got = lax.all_to_all(send, "seq", 0, 0, tiled=True)
    starts = pl.pallas_call(
        scan_kernel,
        out_shape=jax.ShapeDtypeStruct((count, N // 2, SLAB), bf16),
        in_specs=whole(1),
        out_specs=whole(1)[0],
        name="carry",
    )(got)
    state = lax.all_to_all(starts, "seq", 0, 0, tiled=True).reshape(slabs, N, SLAB)

    within = pl.pallas_call(
        within_kernel,
        out_shape=jax.ShapeDtypeStruct((height, width), f32),
        in_specs=whole(5),
        out_specs=whole(1)[0],
        name="within",
    )(xc, bcv, cols, lines, jnp.repeat(d_skip, P_SIZE)[None])

    ready = pl.pallas_call(
        gate_kernel,
        out_shape=jax.ShapeDtypeStruct((height + TAIL, width), bf16),
        in_specs=whole(6),
        out_specs=whole(1)[0],
        name="gate",
    )(within, state, bcv, cols, z_in, norm_gain[None])

    def around(value, distance):
        return lax.ppermute(value, "head", [((i + distance) % fans, i) for i in range(fans)])

    def swapped(value):
        return lax.ppermute(value, "dp", [(0, 1), (1, 0)])

    ahead = around(ready, 1)
    behind = around(ready, -1)
    far_top = around(ahead[: height // 2], 1)
    far_end = around(behind[height // 2 :], -1)
    near = [ready, ahead, behind, far_top, far_end]
    other = [swapped(value) for value in near]
    away = jnp.array([0, 1, 3, 2], jnp.int32)
    place = jnp.concatenate([(2 * mine - away) % 8, (2 * mine + 1 + away) % 8])
    share = out_weight.shape[1] * count // fans
    here, there = pl.pallas_call(
        project_kernel,
        grid_spec=pltpu.PrefetchScalarGridSpec(
            num_scalar_prefetch=1,
            grid=(fans,),
            in_specs=[pl.BlockSpec(memory_space=pl.ANY)] * 10
            + [
                pl.BlockSpec((depth, share // 2), lambda k, s: (0, s[k])),
                pl.BlockSpec((depth, share // 2), lambda k, s: (0, s[4 + k])),
            ],
            out_specs=[pl.BlockSpec((height, share // 2), lambda k, s: (0, 0))] * 2,
            scratch_shapes=[pltpu.VMEM((height, share // 2), f32)] * 2
            + [pltpu.VMEM((4, 2, height + 2 * TAIL, width), bf16), pltpu.SemaphoreType.DMA((2, 5))],
        ),
        out_shape=[jax.ShapeDtypeStruct((height, share // 2), bf16)] * 2,
        name="project",
    )(place.astype(jnp.int32), *near, *other, weights, weights)

    return pl.pallas_call(
        finish_kernel,
        out_shape=jax.ShapeDtypeStruct((height, share), bf16),
        in_specs=[pl.BlockSpec(memory_space=pltpu.SMEM)] + whole(2),
        out_specs=whole(1)[0],
        name="finish",
    )(core.astype(jnp.int32)[None], here, swapped(there))


def solution(mesh):
    placed = (
        P(("dp", "seq"), "head"),
        P(("dp", "seq"), "head"),
        P(("dp", "seq"), "head"),
        P(("dp", "seq"), "head"),
        P("head"),
        P("head"),
        P("head"),
        P(None, "head"),
        P(None, "head"),
        P("head"),
        P("head", "seq"),
    )
    return jax.shard_map(
        layer, mesh=mesh, in_specs=placed, out_specs=P(("dp", "seq"), "head"), check_vma=False
    )
```

```python
import jax
import jax.numpy as jnp
from jax import lax
from jax.experimental import pallas as pl
from jax.experimental.pallas import tpu as pltpu
from jax.sharding import PartitionSpec as P


H = 128
P_SIZE = 64
N = 128
BLOCK = 256
CONV = 4
SLAB = 128
HALO = 8
TAIL = 8
EPSILON = 1e-05


bf16 = jnp.bfloat16
f32 = jnp.float32


def pieces_of(value):
    high = value.astype(bf16)
    rest = value - high.astype(f32)
    middle = rest.astype(bf16)
    low = (rest - middle.astype(f32)).astype(bf16)
    return high, middle, low


def silu(value):
    return value / (1.0 + jnp.exp(-value))


def convolved(halo, current, taps):
    joined = jnp.concatenate([halo.astype(f32), current.astype(f32)], axis=0)
    height = current.shape[0]
    first = HALO - (CONV - 1)
    summed = taps[0:1] * joined[first : first + height]
    for k in range(1, CONV):
        summed = summed + taps[k : k + 1] * joined[first + k : first + k + height]
    return silu(summed).astype(bf16)


def spread_pair(left, right, rows):
    lane = lax.broadcasted_iota(jnp.int32, (rows, SLAB), 1)
    return jnp.where(
        lane < P_SIZE,
        jnp.broadcast_to(left, (rows, SLAB)),
        jnp.broadcast_to(right, (rows, SLAB)),
    )


def front_kernel(
    x_ref, bc_ref, halo_ref, dt_ref, bias_ref, alog_ref, tapx_ref, tapbc_ref,
    xc_ref, bcv_ref, col_ref, row_ref, send_ref,
):
    heads = dt_ref.shape[0]
    width = x_ref.shape[1]
    diagonal = lax.broadcasted_iota(jnp.int32, (heads, heads), 0) == lax.broadcasted_iota(
        jnp.int32, (heads, heads), 1
    )

    def stood(line):
        square = jnp.broadcast_to(line, (heads, heads))
        return jnp.sum(jnp.where(diagonal, square, 0.0), axis=1, keepdims=True)

    raw = dt_ref[...] + stood(bias_ref[...])
    step = jnp.maximum(raw, 0.0) + jnp.log1p(jnp.exp(-jnp.abs(raw)))
    running = -jnp.exp(stood(alog_ref[...])) * step
    lane = lax.broadcasted_iota(jnp.int32, running.shape, 1)
    shift = 1
    while shift < BLOCK:
        moved = pltpu.roll(running, shift, 1)
        running = running + jnp.where(lane >= shift, moved, 0.0)
        shift *= 2
    finish = jnp.exp(running[:, BLOCK - 1 : BLOCK] - running) * step
    row_ref[0:heads] = running
    row_ref[heads : 2 * heads] = step
    columns = jnp.concatenate([running, step, finish, jnp.exp(running)], axis=0).T
    col_ref[...] = columns

    groups = bc_ref.shape[1] // (2 * N)
    turned = []
    for g in range(2 * groups):
        at = slice(g * N, (g + 1) * N)
        here = convolved(halo_ref[:, width + g * N : width + (g + 1) * N], bc_ref[:, at], tapbc_ref[:, at])
        bcv_ref[:, at] = here
        if g % 2 == 0:
            turned.append(here.astype(f32).T.astype(bf16))
    slabs = width // SLAB
    for c in range(slabs):
        at = slice(c * SLAB, (c + 1) * SLAB)
        here = convolved(halo_ref[:, at], x_ref[:, at], tapx_ref[:, at])
        xc_ref[:, at] = here
        h = 2 * c
        weight = spread_pair(
            columns[:, 2 * heads + h : 2 * heads + h + 1],
            columns[:, 2 * heads + h + 1 : 2 * heads + h + 2],
            BLOCK,
        )
        weighted = (here.astype(f32) * weight).astype(bf16)
        fresh = jnp.dot(turned[c // (slabs // groups)], weighted, preferred_element_type=f32)
        decay = spread_pair(
            columns[BLOCK - 1 : BLOCK, 3 * heads + h : 3 * heads + h + 1],
            columns[BLOCK - 1 : BLOCK, 3 * heads + h + 1 : 3 * heads + h + 2],
            8,
        )
        high, middle, low = pieces_of(decay)
        sub = lax.broadcasted_iota(jnp.int32, (8, SLAB), 0)
        lines = jnp.where(
            sub == 0, high.astype(f32), jnp.where(sub == 1, middle.astype(f32), low.astype(f32))
        ).astype(bf16)
        send_ref[2 * c, 0 : N // 2] = fresh[0 : N // 2].astype(bf16)
        send_ref[2 * c + 1, 0 : N // 2] = fresh[N // 2 : N].astype(bf16)
        send_ref[2 * c, N // 2 : N // 2 + 8] = lines
        send_ref[2 * c + 1, N // 2 : N // 2 + 8] = lines


def scan_kernel(got_ref, start_ref):
    count = got_ref.shape[0]
    rows = start_ref.shape[1]

    def advance(j, state):
        start_ref[j] = state.astype(bf16)
        block = got_ref[j].astype(f32)
        decay = block[rows : rows + 1] + block[rows + 1 : rows + 2] + block[rows + 2 : rows + 3]
        return decay * state + block[0:rows]

    lax.fori_loop(0, count, advance, jnp.zeros((rows, SLAB), f32))


def within_kernel(xc_ref, bcv_ref, col_ref, row_ref, skip_ref, out_ref):
    heads = row_ref.shape[0] // 2
    slabs = xc_ref.shape[1] // SLAB
    groups = bcv_ref.shape[1] // (2 * N)
    half = BLOCK // 2
    lane = lax.broadcasted_iota(jnp.int32, (half, SLAB), 1)
    sub = lax.broadcasted_iota(jnp.int32, (half, half), 0)
    across_lane = lax.broadcasted_iota(jnp.int32, (half, half), 1)
    keep = sub >= across_lane
    for g in range(groups):
        b_here = bcv_ref[:, 2 * g * N : (2 * g + 1) * N]
        c_here = bcv_ref[:, (2 * g + 1) * N : (2 * g + 2) * N]
        scores = lax.dot_general(
            c_here, b_here, (((1,), (1,)), ((), ())), preferred_element_type=f32
        )
        for c in range(g * slabs // groups, (g + 1) * slabs // groups):
            at = slice(c * SLAB, (c + 1) * SLAB)
            x_here = xc_ref[:, at]
            parts = []
            for h in (2 * c, 2 * c + 1):
                run_row = row_ref[h : h + 1]
                step_row = row_ref[heads + h : heads + h + 1]
                run_col = jnp.broadcast_to(col_ref[:, h : h + 1], (BLOCK, half))

                def mix(i, j, run_col=run_col, run_row=run_row, step_row=step_row):
                    ri = slice(i * half, (i + 1) * half)
                    rj = slice(j * half, (j + 1) * half)
                    spread = run_col[ri] - run_row[:, rj]
                    if i == j:
                        spread = jnp.where(keep, spread, -jnp.inf)
                    return (scores[ri, rj] * jnp.exp(spread) * step_row[:, rj]).astype(bf16)

                upper = jnp.dot(mix(0, 0), x_here[0:half], preferred_element_type=f32)
                lower = jnp.dot(
                    jnp.concatenate([mix(1, 0), mix(1, 1)], axis=1),
                    x_here,
                    preferred_element_type=f32,
                )
                parts.append((upper, lower))
            skip = skip_ref[:, at]
            for i in range(2):
                ri = slice(i * half, (i + 1) * half)
                out_ref[ri, at] = (
                    jnp.where(lane < P_SIZE, parts[0][i], parts[1][i])
                    + skip * x_here[ri].astype(f32)
                )


def gate_kernel(within_ref, state_ref, bcv_ref, col_ref, z_ref, gain_ref, out_ref):
    heads = col_ref.shape[1] // 4
    slabs = within_ref.shape[1] // SLAB
    groups = bcv_ref.shape[1] // (2 * N)
    squares = jnp.zeros((BLOCK, SLAB), f32)
    for c in range(slabs):
        at = slice(c * SLAB, (c + 1) * SLAB)
        g = c // (slabs // groups)
        c_here = bcv_ref[:, (2 * g + 1) * N : (2 * g + 2) * N]
        across = jnp.dot(c_here, state_ref[c], preferred_element_type=f32)
        h = 3 * heads + 2 * c
        grown = spread_pair(col_ref[:, h : h + 1], col_ref[:, h + 1 : h + 2], BLOCK)
        mixed = within_ref[:, at] + across * grown
        gated = mixed * silu(z_ref[:, at].astype(f32))
        squares = squares + gated * gated
        out_ref[0:BLOCK, at] = (gated * gain_ref[:, at]).astype(bf16)
    line = lax.dot_general(
        jnp.ones((TAIL, SLAB), f32),
        squares,
        (((1,), (1,)), ((), ())),
        preferred_element_type=f32,
        precision=lax.Precision.HIGHEST,
    )
    end = slice(BLOCK, BLOCK + TAIL)
    for i, piece in enumerate(pieces_of(line)):
        out_ref[end, i * BLOCK : (i + 1) * BLOCK] = piece
    rest = within_ref.shape[1] - 3 * BLOCK
    out_ref[end, 3 * BLOCK :] = jnp.zeros((TAIL, rest), bf16)


def project_kernel(place_ref, *refs):
    sides = (refs[0:5], refs[5:10])
    w_refs = refs[10:12]
    outs = refs[12:14]
    total, left_ref, tail_ref, done = refs[14:18]
    k = pl.program_id(0)
    half = BLOCK // 2
    bodies, tails = [], []
    for n, side in enumerate(sides):
        first = n * BLOCK
        rows = [(i, 0, BLOCK, first) for i in range(3)]
        rows += [(3, 0, half, first), (4, 0, half, first + half)]
        for i, (ref, start, count, at) in enumerate(rows):
            step = min(i, 3)
            bodies.append(
                (step, pltpu.make_async_copy(
                    side[ref].at[pl.ds(start, count)],
                    left_ref.at[step, pl.ds(at, count)],
                    done.at[n, i],
                ))
            )
        for step, (ref, start) in enumerate(((0, BLOCK), (1, BLOCK), (2, BLOCK), (4, half))):
            tails.append(
                pltpu.make_async_copy(
                    side[ref].at[pl.ds(start, TAIL)], tail_ref.at[step, n], done.at[n, 5 + step]
                )
            )

    @pl.when(k == 0)
    def _():
        for step in range(4):
            for own, copy in bodies:
                if own == step:
                    copy.start()
        for copy in tails:
            copy.start()
        total[...] = jnp.zeros(total.shape, f32)

    for step in range(4):

        @pl.when(k == step)
        def _(step=step):
            for own, copy in bodies:
                if own == step:
                    copy.wait()

    weight = jnp.concatenate(
        [
            jnp.concatenate(
                [
                    w_ref[:, (2 * j + r) * SLAB : (2 * j + r + 1) * SLAB]
                    for w_ref in w_refs
                    for j in range(2)
                ],
                axis=1,
            )
            for r in range(2)
        ],
        axis=0,
    )
    total[...] = total[...] + jnp.dot(left_ref[k], weight, preferred_element_type=f32)

    @pl.when(k == 3)
    def _():
        for copy in tails:
            copy.wait()
        for n, out in enumerate(outs):
            line = jnp.zeros((TAIL, BLOCK), f32)
            for step in range(4):
                for i in range(3):
                    line = line + tail_ref[step, n, :, i * BLOCK : (i + 1) * BLOCK].astype(f32)
            scale = lax.rsqrt(line / (H * P_SIZE) + EPSILON)
            column = jnp.concatenate([scale] * (SLAB // TAIL), axis=0).T[:, 0:1]
            out[...] = (total[n * BLOCK : (n + 1) * BLOCK] * column).astype(bf16)


def finish_kernel(core_ref, mine_ref, theirs_ref, out_ref):
    core = core_ref[0]
    for j in range(mine_ref.shape[1] // SLAB):
        at = slice(j * SLAB, (j + 1) * SLAB)
        mine = pl.multiple_of((2 * j + core) * SLAB, SLAB)
        theirs = pl.multiple_of((2 * j + 1 - core) * SLAB, SLAB)
        out_ref[:, pl.ds(mine, SLAB)] = mine_ref[:, at]
        out_ref[:, pl.ds(theirs, SLAB)] = theirs_ref[:, at]


def seat_of(h, half, x):
    away = (x - h) % 4
    return (2 * h + (1 + away if half else -away)) % 8


def weight_route(fans):
    ring = 4
    route = []
    for h in range(fans):
        for half in range(2):
            for x in range(fans):
                for y in range(ring):
                    for core in range(2):
                        source = (((2 * h + half) * ring + y) * fans + x) * 2 + core
                        seat = seat_of(h, half, x) * ring + 2 * (y // 2) + core
                        route.append((source, (seat * fans + h) * 2 + y % 2))
    return route


def whole(count):
    return [pl.BlockSpec(memory_space=pltpu.VMEM) for _ in range(count)]


def layer(
    x_in, bc_in, z_in, dt_raw, dt_bias, a_log, d_skip, conv_x, conv_bc, norm_gain, out_weight
):
    height, width = x_in.shape
    heads = dt_raw.shape[1]
    nearby = bc_in.shape[1]
    slabs = width // SLAB
    count = lax.axis_size("seq")
    fans = lax.axis_size("head")
    core = lax.axis_index("dp")
    mine = lax.axis_index("head")

    tail = jnp.concatenate([x_in[height - HALO :], bc_in[height - HALO :]], axis=1)
    halo = lax.ppermute(tail, "seq", [(i, i + 1) for i in range(count - 1)])

    depth = width // 2
    piece = lax.dynamic_slice_in_dim(out_weight, core * depth, depth, 0)
    piece = lax.ppermute(piece, ("seq", "head", "dp"), weight_route(fans))

    xc, bcv, cols, lines, send = pl.pallas_call(
        front_kernel,
        out_shape=(
            jax.ShapeDtypeStruct((height, width), bf16),
            jax.ShapeDtypeStruct((height, nearby), bf16),
            jax.ShapeDtypeStruct((height, 4 * heads), f32),
            jax.ShapeDtypeStruct((2 * heads, height), f32),
            jax.ShapeDtypeStruct((2 * slabs, N // 2 + 8, SLAB), bf16),
        ),
        in_specs=whole(8),
        out_specs=tuple(whole(5)),
        name="front",
    )(x_in, bc_in, halo, dt_raw.T, dt_bias[None], a_log[None], conv_x, conv_bc)

    weights = lax.all_gather(piece, "seq", axis=1, tiled=True)
    got = lax.all_to_all(send, "seq", 0, 0, tiled=True)
    starts = pl.pallas_call(
        scan_kernel,
        out_shape=jax.ShapeDtypeStruct((count, N // 2, SLAB), bf16),
        in_specs=whole(1),
        out_specs=whole(1)[0],
        name="carry",
    )(got)
    state = lax.all_to_all(starts, "seq", 0, 0, tiled=True).reshape(slabs, N, SLAB)

    within = pl.pallas_call(
        within_kernel,
        out_shape=jax.ShapeDtypeStruct((height, width), f32),
        in_specs=whole(5),
        out_specs=whole(1)[0],
        name="within",
    )(xc, bcv, cols, lines, jnp.repeat(d_skip, P_SIZE)[None])

    ready = pl.pallas_call(
        gate_kernel,
        out_shape=jax.ShapeDtypeStruct((height + TAIL, width), bf16),
        in_specs=whole(6),
        out_specs=whole(1)[0],
        name="gate",
    )(within, state, bcv, cols, z_in, norm_gain[None])

    def around(value, distance):
        return lax.ppermute(value, "head", [((i + distance) % fans, i) for i in range(fans)])

    def swapped(value):
        return lax.ppermute(value, "dp", [(0, 1), (1, 0)])

    ahead = around(ready, 1)
    behind = around(ready, -1)
    far_top = around(ahead[: height // 2], 1)
    far_end = around(behind[height // 2 :], -1)
    near = [ready, ahead, behind, far_top, far_end]
    other = [swapped(value) for value in near]
    away = jnp.array([0, 1, 3, 2], jnp.int32)
    place = jnp.concatenate([(2 * mine - away) % 8, (2 * mine + 1 + away) % 8])
    share = out_weight.shape[1] * count // fans
    here, there = pl.pallas_call(
        project_kernel,
        grid_spec=pltpu.PrefetchScalarGridSpec(
            num_scalar_prefetch=1,
            grid=(fans,),
            in_specs=[pl.BlockSpec(memory_space=pl.ANY)] * 10
            + [
                pl.BlockSpec((depth, share // 2), lambda k, s: (0, s[k])),
                pl.BlockSpec((depth, share // 2), lambda k, s: (0, s[4 + k])),
            ],
            out_specs=[pl.BlockSpec((height, share // 2), lambda k, s: (0, 0))] * 2,
            scratch_shapes=[
                pltpu.VMEM((2 * height, share // 2), f32),
                pltpu.VMEM((4, 2 * height, width), bf16),
                pltpu.VMEM((4, 2, TAIL, width), bf16),
                pltpu.SemaphoreType.DMA((2, 9)),
            ],
        ),
        out_shape=[jax.ShapeDtypeStruct((height, share // 2), bf16)] * 2,
        name="project",
    )(place.astype(jnp.int32), *near, *other, weights, weights)

    return pl.pallas_call(
        finish_kernel,
        out_shape=jax.ShapeDtypeStruct((height, share), bf16),
        in_specs=[pl.BlockSpec(memory_space=pltpu.SMEM)] + whole(2),
        out_specs=whole(1)[0],
        name="finish",
    )(core.astype(jnp.int32)[None], here, swapped(there))


def solution(mesh):
    placed = (
        P(("dp", "seq"), "head"),
        P(("dp", "seq"), "head"),
        P(("dp", "seq"), "head"),
        P(("dp", "seq"), "head"),
        P("head"),
        P("head"),
        P("head"),
        P(None, "head"),
        P(None, "head"),
        P("head"),
        P("head", "seq"),
    )
    return jax.shard_map(
        layer, mesh=mesh, in_specs=placed, out_specs=P(("dp", "seq"), "head"), check_vma=False
    )
```
